128 devices in a mesh: row: 4 (over z_hi, core), col: 32 (over z_lo, x, y).
Axes of the slice: x: 4, y: 4, z: 4 (z_hi: 2, z_lo: 2; z = z_hi * 2 + z_lo), core: 2. Of those that a mesh axis runs over, the one named last changes fastest.
Arguments:
- derivs: bfloat16 [1024, 65536], P(('row', 'col')), may hold values from -15 to 15, as said below
- energy_derivs: bfloat16 [1024, 65536], P(('row', 'col')), may hold values from -15 to 15, as said below
- energies: float32 [1024], P(('row', 'col')), may hold values from -30 to -10, as said below
Outputs:
- correlation: float32 [4096, 65536], P('row', 'col')
- hamiltonian: float32 [4096, 65536], P('row', 'col')
The draws below stay inside these ranges and needn't reach their ends.
Inputs may be any that keep to these rules, and one draw needn't show every extreme that they name: `derivs`: finite values. `energy_derivs`: finite values. `energies`: finite values.
All inputs are finite; a program needn't handle non-finite values.
Results may differ from the reference program's by a relative error of at most 0.0041.
Values may be sent and summed in bfloat16 or wider, within the bound.
A program may use at most 128 MiB of HBM per device.

```python
import math
import jax
import jax.numpy as jnp
from jax import lax

P_SIZE = 65536
SLAB = 4096
NS = 1024


def trend_weights():
    positions = jnp.arange(NS, dtype=jnp.float32)
    return 0.5 + positions / (NS - 1)


def sample_block(seed_key):
    keys = jax.random.split(seed_key, 3)
    scales = jnp.exp(jax.random.uniform(keys[0], (P_SIZE,), jnp.float32, math.log(0.3), math.log(3.0)))
    offsets = jax.random.uniform(keys[1], (P_SIZE,), jnp.float32, -1.5, 1.5)
    noise = jnp.clip(jax.random.normal(keys[2], (NS, P_SIZE), jnp.float32), -4.0, 4.0)
    values = trend_weights()[:, None] * offsets[None, :] + noise * scales[None, :]
    return values.astype(jnp.bfloat16)


def draw_derivs(key, part):
    return sample_block(jax.random.fold_in(key, 101))


def draw_energy_derivs(key, part):
    return sample_block(jax.random.fold_in(key, 202))


def draw_energies(key, part):
    seed_key = jax.random.fold_in(key, 303)
    noise = jnp.clip(jax.random.normal(seed_key, (NS,), jnp.float32), -4.0, 4.0)
    return -20.0 + 3.0 * trend_weights() + noise


def setup_inputs(seed: int = 0) -> dict:
    key_list = jax.random.split(jax.random.key(seed), 4)
    derivs = draw_derivs(jax.random.fold_in(key_list[3], 71), 0)
    energy_derivs = draw_energy_derivs(jax.random.fold_in(key_list[3], 71), 0)
    energies = draw_energies(jax.random.fold_in(key_list[3], 71), 0)
    return {"derivs": derivs, "energy_derivs": energy_derivs, "energies": energies}


def reference(derivs, energy_derivs, energies):
    total_count = derivs.shape[0]
    derivs_full = derivs.astype(jnp.float32)
    grads_full = energy_derivs.astype(jnp.float32)
    mean_derivs = jnp.sum(derivs_full, axis=0) / total_count
    mean_grads = jnp.sum(grads_full, axis=0) / total_count
    mean_energy = jnp.sum(energies) / total_count
    offsets = derivs_full - mean_derivs[None, :]
    centred = offsets.astype(jnp.bfloat16)
    energy_term = ((energies - mean_energy)[:, None] * offsets + (grads_full - mean_grads[None, :])).astype(jnp.bfloat16)
    row_block = centred[:, :SLAB]
    width = min(P_SIZE, 4096)
    blocks = P_SIZE // width
    centred_blocks = centred.reshape(total_count, blocks, width).transpose(1, 0, 2)
    term_blocks = energy_term.reshape(total_count, blocks, width).transpose(1, 0, 2)

    def one_block(pair_blocks):
        left = lax.dot_general(row_block, pair_blocks[0], (((0,), (0,)), ((), ())), preferred_element_type=jnp.float32)
        right = lax.dot_general(row_block, pair_blocks[1], (((0,), (0,)), ((), ())), preferred_element_type=jnp.float32)
        return left, right

    over_blocks, hamil_blocks = lax.map(one_block, (centred_blocks, term_blocks))
    correlation = over_blocks.transpose(1, 0, 2).reshape(SLAB, P_SIZE) / total_count
    hamiltonian = hamil_blocks.transpose(1, 0, 2).reshape(SLAB, P_SIZE) / total_count
    return correlation, hamiltonian
```

```python
import functools

import jax
import jax.numpy as jnp
from jax import lax
from jax.experimental import pallas as pl
from jax.experimental.pallas import tpu as pltpu
from jax.sharding import PartitionSpec as P

MESH = pl.DeviceIdType.MESH
LANES = 128
WIDTH = 128
TAIL = 4
F32 = jnp.float32
BF16 = jnp.bfloat16


def place():
    row, col = lax.axis_index("row"), lax.axis_index("col")
    x, y = (col // 4) % 4, col % 4
    return x, y, (row // 2) * 2 + col // 16, row % 2


def device(x, y, z, core):
    return {"row": (z // 2) * 2 + core, "col": (z % 2) * 16 + x * 4 + y}


def send(src, dst, send_sem, recv_sem, target):
    pltpu.make_async_remote_copy(
        src, dst, send_sem, recv_sem, device_id=device(*target), device_id_type=MESH
    ).start()


def keep(src, dst, sem):
    pltpu.make_async_copy(src, dst, sem).start()


def await_bytes(ref, sem):
    pltpu.make_async_copy(ref, ref, sem).wait()


def multiply(k, tiles, row_t, weight, mixed, store):
    total = 1024
    width = tiles.shape[-1]

    def add_up(i, sums):
        core, y = i // 4, i % 4
        return tuple(
            s + tiles[k, core, y, :, a].astype(F32).reshape(16, 8, width).sum(axis=0)
            for a, s in enumerate(sums)
        )

    zero = jnp.zeros((8, width), F32)
    sums = lax.fori_loop(0, 8, add_up, (zero, zero), unroll=True)
    means = [s.sum(axis=0, keepdims=True) / total for s in sums]

    def centre(i, _):
        core, y = i // 4, i % 4
        offset = tiles[k, core, y, :, 0].astype(F32).reshape(128, width) - means[0]
        grad = tiles[k, core, y, :, 1].astype(F32).reshape(128, width) - means[1]
        rows = pl.ds(pl.multiple_of(i * 128, 128), 128)
        mixed[rows, 0:width] = offset.astype(BF16)
        mixed[rows, width : 2 * width] = (weight[rows, :] * offset + grad).astype(BF16)
        return 0

    lax.fori_loop(0, 8, centre, 0)

    def part(i, _):
        rows = pl.ds(pl.multiple_of(i * 256, 256), 256)
        store(rows, jnp.dot(row_t[rows, :], mixed[...], preferred_element_type=F32) / total)
        return 0

    lax.fori_loop(0, 4, part, 0)


def exchange(
    derivs, grads, energy, tiles, row_t, weight, done,
    zb, xb, r0, ra, rb, ez, ex, ey, mixed,
    s_z, s_x, s_y, s_c, s_r, s_e, z_sem, x_sem, y_sem, c_sem, r_sem, e_sem,
):
    x, y, z, core = place()
    chunks = tiles.shape[0]
    quarter = chunks // 4
    early = done.shape[0]
    mates = [(x, y, (z + d) % 4, core) for d in (2, 1, 3)]
    others = [(x, y, (z + d) % 4, 1 - core) for d in (0, 2, 1, 3)]
    along_x = [((x + d) % 4, y, z, core) for d in (2, 1, 3)]
    along_y = [(x, (y + d) % 4, z, core) for d in (2, 1, 3)]
    partner = (x, y, z, 1 - core)

    barrier = pltpu.get_barrier_semaphore()
    for peer in mates + others + along_x + along_y:
        pl.semaphore_signal(barrier, 1, device_id=device(*peer), device_id_type=MESH)
    pl.semaphore_wait(barrier, 13)

    for group, sem in ((mates, 0), (others, 1)):
        for peer in group:
            block = derivs.at[0, 0, peer[2] // 2, pl.ds(peer[3] * 2, 2)]
            send(block, r0.at[core, z], s_r.at[sem], r_sem.at[0], peer)
    keep(derivs.at[0, 0, z // 2, pl.ds(core * 2, 2)], r0.at[core, z], r_sem.at[0])
    for peer in mates:
        send(energy, ez.at[z], s_e.at[0], e_sem.at[0], peer)
    keep(energy, ez.at[z], e_sem.at[0])

    @pl.loop(0, chunks)
    def _(k):
        for a, source in enumerate((derivs, grads)):
            for peer in mates:
                block = source.at[peer[2] % 2, :, :, k // quarter, k % quarter]
                send(block, zb.at[k, :, :, a, z], s_z, z_sem.at[k], peer)
            block = source.at[z % 2, :, :, k // quarter, k % quarter]
            keep(block, zb.at[k, :, :, a, z], z_sem.at[k])

    await_bytes(r0, r_sem.at[0])
    for peer in along_x:
        send(r0.at[:, :, 0], ra.at[y, x], s_r.at[2], r_sem.at[1], peer)
    keep(r0.at[:, :, 0], ra.at[y, x], r_sem.at[1])
    for peer in along_y:
        send(r0.at[:, :, 1], rb.at[x, y], s_r.at[3], r_sem.at[2], peer)
    keep(r0.at[:, :, 1], rb.at[x, y], r_sem.at[2])
    await_bytes(ez, e_sem.at[0])
    for peer in along_x:
        send(ez, ex.at[x], s_e.at[1], e_sem.at[1], peer)
    keep(ez, ex.at[x], e_sem.at[1])
    await_bytes(ra.at[y], r_sem.at[1])
    for peer in along_y:
        send(ra.at[y], ra.at[y], s_r.at[4], r_sem.at[3], peer)
    await_bytes(rb.at[x], r_sem.at[2])
    for peer in along_x:
        send(rb.at[x], rb.at[x], s_r.at[5], r_sem.at[4], peer)
    await_bytes(ex, e_sem.at[1])
    for peer in along_y:
        send(ex, ey.at[core, y], s_e.at[2], e_sem.at[2], peer)
    keep(ex, ey.at[core, y], e_sem.at[2])

    def to_x(k):
        await_bytes(zb.at[k], z_sem.at[k])
        for peer in along_x:
            send(zb.at[k, peer[0]], xb.at[k, :, x], s_x, x_sem.at[k], peer)
        keep(zb.at[k, x], xb.at[k, :, x], x_sem.at[k])

    def to_y(k):
        await_bytes(xb.at[k], x_sem.at[k])
        for peer in along_y:
            send(xb.at[k, peer[1]], tiles.at[k, core, y], s_y, y_sem.at[k], peer)
        keep(xb.at[k, y], tiles.at[k, core, y], y_sem.at[k])

    def to_partner(k):
        await_bytes(tiles.at[k, core], y_sem.at[k])
        send(tiles.at[k, core], tiles.at[k, core], s_c, c_sem.at[k], partner)

    def finish(k):
        await_bytes(tiles.at[k, 1 - core], c_sem.at[k])

        def store(rows, value):
            done[k, rows, :] = value

        multiply(k, tiles, row_t, weight, mixed, store)

    first = 5

    @pl.loop(0, first)
    def _(k):
        to_x(k)

        @pl.when(k >= 1)
        def _():
            to_y(k - 1)

        @pl.when(k >= 2)
        def _():
            to_partner(k - 2)

    await_bytes(ey.at[core], e_sem.at[2])
    send(ey.at[core], ey.at[core], s_e.at[3], e_sem.at[3], partner)

    await_bytes(ra.at[0:3], r_sem.at[3])
    await_bytes(rb.at[0:3], r_sem.at[4])

    @pl.loop(0, quarter)
    def _(c):
        for half, source in enumerate((ra, rb)):
            blocks = []
            for i in range(8):
                if half == 0:
                    block = source[i % 4, :, i // 4, :, c]
                else:
                    block = source[:, i % 4, i // 4, :, c]
                blocks.append(block.astype(F32).reshape(128, LANES))
            total = sum(b.reshape(16, 8, LANES).sum(axis=0) for b in blocks)
            mean = total.sum(axis=0, keepdims=True) / 1024
            rows = pl.ds(pl.multiple_of((half * quarter + c) * LANES, LANES), LANES)
            for i, block in enumerate(blocks):
                row_t[rows, i * 128 : (i + 1) * 128] = (block - mean).T.astype(BF16)

    await_bytes(ey.at[1 - core], e_sem.at[3])
    every = ey[...].reshape(1024, LANES)
    mean_energy = every.reshape(128, 8, LANES).sum(axis=0).sum(axis=0, keepdims=True) / 1024
    weight[...] = every - mean_energy

    @pl.loop(first, chunks)
    def _(k):
        to_x(k)
        to_y(k - 1)
        to_partner(k - 2)
        finish(k - first)

    to_y(chunks - 1)
    to_partner(chunks - 2)
    if chunks - first < early:
        finish(chunks - first)
    to_partner(chunks - 1)
    if chunks - first + 1 < early:
        pl.loop(chunks - first + 1, early)(finish)
    pl.loop(early, chunks)(lambda k: await_bytes(tiles.at[k, 1 - core], c_sem.at[k]))

    await_bytes(zb.at[:, 0:3], s_z)
    await_bytes(xb.at[:, 0:3], s_x)
    await_bytes(tiles.at[:, 0, 0:3], s_y)
    await_bytes(tiles.at[:, 0], s_c)
    await_bytes(r0.at[0, 0:3], s_r.at[0])
    await_bytes(r0.at[0], s_r.at[1])
    await_bytes(ra.at[0, 0:3], s_r.at[2])
    await_bytes(rb.at[0, 0:3], s_r.at[3])
    await_bytes(ra.at[0:3], s_r.at[4])
    await_bytes(rb.at[0:3], s_r.at[5])
    await_bytes(ez.at[0:3], s_e.at[0])
    await_bytes(ex.at[0:3], s_e.at[1])
    await_bytes(ey.at[0, 0:3], s_e.at[2])
    await_bytes(ey.at[0], s_e.at[3])


def write(tiles, row_t, weight, done, corr, hamil, late, mixed, sem):
    chunks, early = tiles.shape[0], done.shape[0]
    outs = (corr, hamil)

    def put(source, k):
        for a, out in enumerate(outs):
            columns = pl.ds(pl.multiple_of(k * LANES, LANES), LANES)
            keep(source.at[:, a * LANES : (a + 1) * LANES], out.at[:, columns], sem.at[a])

    pl.loop(0, early)(lambda k: put(done.at[k], k))

    @pl.loop(early, chunks)
    def _(k):
        def store(rows, value):
            late[k - early, rows, :] = value

        multiply(k, tiles, row_t, weight, mixed, store)
        put(late.at[k - early], k)

    for a, out in enumerate(outs):
        await_bytes(out, sem.at[a])


def body(derivs, grads, energies):
    chunks = 2048 // WIDTH
    early = chunks - TAIL
    quarter = chunks // 4

    def view(a):
        return a.reshape(8, 2, 4, 4, 4, quarter, WIDTH).transpose(1, 2, 3, 4, 5, 0, 6)

    energy = jnp.broadcast_to(energies[:, None], (8, LANES))
    hbm = pl.BlockSpec(memory_space=pl.ANY)
    vmem = pl.BlockSpec(memory_space=pltpu.VMEM)
    dma = pltpu.SemaphoreType.DMA
    tiles, row_t, weight, done = pl.pallas_call(
        exchange,
        out_shape=(
            pltpu.VMEM((chunks, 2, 4, 4, 2, 4, 8, WIDTH), BF16),
            pltpu.VMEM((1024, 1024), BF16),
            pltpu.VMEM((1024, LANES), F32),
            pltpu.VMEM((early, 1024, 2 * WIDTH), F32),
        ),
        in_specs=[hbm, hbm, vmem],
        out_specs=(vmem,) * 4,
        scratch_shapes=[
            pltpu.VMEM((chunks, 4, 4, 2, 4, 8, WIDTH), BF16),
            pltpu.VMEM((chunks, 4, 4, 2, 4, 8, WIDTH), BF16),
            pltpu.VMEM((2, 4, 2, quarter, 8, WIDTH), BF16),
            pltpu.VMEM((4, 4, 2, 4, quarter, 8, WIDTH), BF16),
            pltpu.VMEM((4, 4, 2, 4, quarter, 8, WIDTH), BF16),
            pltpu.VMEM((4, 8, LANES), F32),
            pltpu.VMEM((4, 4, 8, LANES), F32),
            pltpu.VMEM((2, 4, 4, 4, 8, LANES), F32),
            pltpu.VMEM((1024, 2 * WIDTH), BF16),
            dma, dma, dma, dma, dma((6,)), dma((4,)),
            dma((chunks,)), dma((chunks,)), dma((chunks,)), dma((chunks,)), dma((5,)), dma((4,)),
        ],
        compiler_params=pltpu.CompilerParams(
            collective_id=0, has_side_effects=True, vmem_limit_bytes=20 << 20
        ),
        name="exchange",
    )(view(derivs), view(grads), energy)
    out = jax.ShapeDtypeStruct((1024, 2048), F32)
    return pl.pallas_call(
        write,
        out_shape=(out, out),
        in_specs=[vmem] * 4,
        out_specs=(hbm, hbm),
        scratch_shapes=[
            pltpu.VMEM((TAIL, 1024, 2 * WIDTH), F32),
            pltpu.VMEM((1024, 2 * WIDTH), BF16),
            dma((2,)),
        ],
        compiler_params=pltpu.CompilerParams(vmem_limit_bytes=8 << 20),
        name="write",
    )(tiles, row_t, weight, done)


def solution(mesh):
    placed = (P(("row", "col"), None), P(("row", "col"), None), P(("row", "col")))
    return jax.shard_map(
        body,
        mesh=mesh,
        in_specs=placed,
        out_specs=(P("row", "col"), P("row", "col")),
        check_vma=False,
    )
```

```python
import functools

import jax
import jax.numpy as jnp
from jax import lax
from jax.experimental import pallas as pl
from jax.experimental.pallas import tpu as pltpu
from jax.sharding import PartitionSpec as P

MESH = pl.DeviceIdType.MESH
LANES = 128
WIDTH = 128
AHEAD = 3
LAG_Y = 2
LAG_Z = 3
SLAB_STEP = 3
FIRST = 11
TAIL = 2
F32 = jnp.float32
BF16 = jnp.bfloat16


def place():
    row, col = lax.axis_index("row"), lax.axis_index("col")
    x, y = (col // 4) % 4, col % 4
    return x, y, (row // 2) * 2 + col // 16, row % 2


def device(x, y, z, core):
    return {"row": (z // 2) * 2 + core, "col": (z % 2) * 16 + x * 4 + y}


def send(src, dst, send_sem, recv_sem, target):
    pltpu.make_async_remote_copy(
        src, dst, send_sem, recv_sem, device_id=device(*target), device_id_type=MESH
    ).start()


def keep(src, dst, sem):
    pltpu.make_async_copy(src, dst, sem).start()


def await_bytes(ref, sem):
    pltpu.make_async_copy(ref, ref, sem).wait()


def multiply(k, tiles, row_t, weight, mixed, store):
    total = 1024
    width = tiles.shape[-1]

    def add_up(i, sums):
        core, z = i // 4, i % 4
        return tuple(
            s + tiles[k, core, z, :, a].astype(F32).reshape(16, 8, width).sum(axis=0)
            for a, s in enumerate(sums)
        )

    zero = jnp.zeros((8, width), F32)
    sums = lax.fori_loop(0, 8, add_up, (zero, zero), unroll=True)
    means = [s.sum(axis=0, keepdims=True) / total for s in sums]

    def centre(i, _):
        core, z = i // 4, i % 4
        offset = tiles[k, core, z, :, 0].astype(F32).reshape(128, width) - means[0]
        grad = tiles[k, core, z, :, 1].astype(F32).reshape(128, width) - means[1]
        rows = pl.ds(pl.multiple_of(i * 128, 128), 128)
        mixed[rows, 0:width] = offset.astype(BF16)
        mixed[rows, width : 2 * width] = (weight[rows, :] * offset + grad).astype(BF16)
        return 0

    lax.fori_loop(0, 8, centre, 0)

    def part(i, _):
        rows = pl.ds(pl.multiple_of(i * 256, 256), 256)
        store(rows, jnp.dot(row_t[rows, :], mixed[...], preferred_element_type=F32) / total)
        return 0

    lax.fori_loop(0, 4, part, 0)


def exchange(
    derivs, grads, energies, tiles, row_t, weight, done,
    energy, xb, yb, r0, ra, rb, ez, ex, ey, mixed,
    s_x, s_y, s_z, s_c, s_r, s_e, x_sem, y_sem, z_sem, c_sem, r_sem, e_sem,
):
    x, y, z, core = place()
    chunks = tiles.shape[0]
    quarter = chunks // 4
    early = done.shape[0]
    mates = [(x, y, (z + d) % 4, core) for d in (2, 1, 3)]
    others = [(x, y, (z + d) % 4, 1 - core) for d in (0, 2, 1, 3)]
    along_x = [((x + d) % 4, y, z, core) for d in (2, 1, 3)]
    along_y = [(x, (y + d) % 4, z, core) for d in (2, 1, 3)]
    partner = (x, y, z, 1 - core)

    own = lax.broadcasted_iota(jnp.int32, (8, 8), 0) == lax.broadcasted_iota(jnp.int32, (8, 8), 1)
    column = jnp.where(own, energies[...], 0).sum(axis=1, keepdims=True)
    energy[...] = jnp.broadcast_to(column, (8, LANES))

    barrier = pltpu.get_barrier_semaphore()
    for peer in mates + others + along_x + along_y:
        pl.semaphore_signal(barrier, 1, device_id=device(*peer), device_id_type=MESH)
    pl.semaphore_wait(barrier, 13)

    @jax.named_scope("to_x")
    def to_x(k):
        for a, source in enumerate((derivs, grads)):
            for peer in along_x:
                block = source.at[:, peer[0], :, k // quarter, k % quarter]
                send(block, xb.at[k, :, :, a, x], s_x, x_sem.at[k], peer)
            block = source.at[:, x, :, k // quarter, k % quarter]
            keep(block, xb.at[k, :, :, a, x], x_sem.at[k])

    @jax.named_scope("to_y")
    def to_y(k):
        await_bytes(xb.at[k], x_sem.at[k])
        for peer in along_y:
            send(xb.at[k, :, peer[1]], yb.at[k, :, y], s_y, y_sem.at[k], peer)
        keep(xb.at[k, :, y], yb.at[k, :, y], y_sem.at[k])

    @jax.named_scope("to_z")
    def to_z(k):
        await_bytes(yb.at[k], y_sem.at[k])
        for peer in mates:
            send(yb.at[k, peer[2] % 2], tiles.at[k, core, z], s_z, z_sem.at[k], peer)
        keep(yb.at[k, z % 2], tiles.at[k, core, z], z_sem.at[k])

    @jax.named_scope("to_partner")
    def to_partner(k):
        await_bytes(tiles.at[k, core], z_sem.at[k])
        send(tiles.at[k, core], tiles.at[k, core], s_c, c_sem.at[k], partner)

    @jax.named_scope("finish")
    def finish(k):
        await_bytes(tiles.at[k, 1 - core], c_sem.at[k])

        def store(rows, value):
            done[k, rows, :] = value

        multiply(k, tiles, row_t, weight, mixed, store)

    def when(condition, stage, k):
        pl.when(condition)(functools.partial(stage, k))

    def finished(i):
        return jnp.clip(jnp.minimum(2 * (i + 1 - FIRST), i - LAG_Y - LAG_Z), 0, early)

    def step(i):
        when(i + AHEAD < chunks, to_x, i + AHEAD)
        when(i < chunks, to_y, i)
        when((i >= LAG_Y) & (i < chunks + LAG_Y), to_z, i - LAG_Y)
        late = i - LAG_Y - LAG_Z
        when((late >= 0) & (late < chunks), to_partner, late)

    to_x(0)
    for group, sem in ((mates, 0), (others, 1)):
        for peer in group:
            block = derivs.at[0, 0, peer[2] // 2, pl.ds(peer[3] * 2, 2)]
            send(block, r0.at[core, z], s_r.at[sem], r_sem.at[0], peer)
    keep(derivs.at[0, 0, z // 2, pl.ds(core * 2, 2)], r0.at[core, z], r_sem.at[0])
    for peer in mates:
        send(energy, ez.at[z], s_e.at[0], e_sem.at[0], peer)
    keep(energy, ez.at[z], e_sem.at[0])
    for k in range(1, AHEAD):
        to_x(k)

    step(0)
    with jax.named_scope("r1"):
        await_bytes(r0, r_sem.at[0])
        for peer in along_x:
            send(r0.at[:, :, 0], ra.at[y, x], s_r.at[2], r_sem.at[1], peer)
        keep(r0.at[:, :, 0], ra.at[y, x], r_sem.at[1])
        for peer in along_y:
            send(r0.at[:, :, 1], rb.at[x, y], s_r.at[3], r_sem.at[2], peer)
        keep(r0.at[:, :, 1], rb.at[x, y], r_sem.at[2])
        await_bytes(ez, e_sem.at[0])
        for peer in along_x:
            send(ez, ex.at[x], s_e.at[1], e_sem.at[1], peer)
        keep(ez, ex.at[x], e_sem.at[1])
    pl.loop(1, SLAB_STEP)(step)
    with jax.named_scope("r2"):
        await_bytes(ra.at[y], r_sem.at[1])
        await_bytes(rb.at[x], r_sem.at[2])
        await_bytes(ex, e_sem.at[1])

    @pl.loop(SLAB_STEP, SLAB_STEP + 4)
    def _(i):
        step(i)
        for side in range(2):
            part = (side, i - SLAB_STEP)
            for peer in along_y:
                send(ra.at[(y, slice(None), *part)], ra.at[(y, slice(None), *part)], s_r.at[4], r_sem.at[3], peer)
            for peer in along_x:
                send(rb.at[(x, slice(None), *part)], rb.at[(x, slice(None), *part)], s_r.at[5], r_sem.at[4], peer)

    for peer in along_y:
        send(ex, ey.at[core, y], s_e.at[2], e_sem.at[2], peer)
    keep(ex, ey.at[core, y], e_sem.at[2])
    pl.loop(SLAB_STEP + 4, FIRST - 1)(step)
    with jax.named_scope("e"):
        await_bytes(ey.at[core], e_sem.at[2])
    send(ey.at[core], ey.at[core], s_e.at[3], e_sem.at[3], partner)
    step(FIRST - 1)

    with jax.named_scope("r3"):
        await_bytes(ra.at[0:3], r_sem.at[3])
        await_bytes(rb.at[0:3], r_sem.at[4])

    @pl.loop(0, quarter)
    @jax.named_scope("prep")
    def _(c):
        for half, source in enumerate((ra, rb)):
            blocks = []
            for i in range(8):
                block = source[:, :, i // 4, i % 4, c].astype(F32)
                if half == 1:
                    block = jnp.stack([block[:, j] for j in range(4)])
                blocks.append(block.reshape(128, LANES))
            total = sum(b.reshape(16, 8, LANES).sum(axis=0) for b in blocks)
            mean = total.sum(axis=0, keepdims=True) / 1024
            rows = pl.ds(pl.multiple_of((half * quarter + c) * LANES, LANES), LANES)
            for i, block in enumerate(blocks):
                row_t[rows, i * 128 : (i + 1) * 128] = (block - mean).T.astype(BF16)

    await_bytes(ey.at[1 - core], e_sem.at[3])
    mean_energy = ey[...].reshape(128, 8, LANES).sum(axis=0).sum(axis=0, keepdims=True) / 1024
    for i in range(8):
        every = ey[i // 4, :, :, i % 4].reshape(128, LANES)
        weight[i * 128 : (i + 1) * 128, :] = every - mean_energy

    @pl.loop(FIRST, chunks + LAG_Y + LAG_Z)
    def _(i):
        step(i)
        pl.loop(finished(i - 1), finished(i))(finish)

    pl.loop(finished(chunks + LAG_Y + LAG_Z - 1), early)(finish)
    pl.loop(early, chunks)(lambda k: await_bytes(tiles.at[k, 1 - core], c_sem.at[k]))

    await_bytes(xb.at[:, :, 0:3], s_x)
    await_bytes(yb.at[:, :, 0:3], s_y)
    await_bytes(tiles.at[:, 0, 0:3], s_z)
    await_bytes(tiles.at[:, 0], s_c)
    await_bytes(r0.at[0, 0:3], s_r.at[0])
    await_bytes(r0.at[0], s_r.at[1])
    await_bytes(ra.at[0, 0:3], s_r.at[2])
    await_bytes(rb.at[0, 0:3], s_r.at[3])
    await_bytes(ra.at[0:3], s_r.at[4])
    await_bytes(rb.at[0:3], s_r.at[5])
    await_bytes(ez.at[0:3], s_e.at[0])
    await_bytes(ex.at[0:3], s_e.at[1])
    await_bytes(ey.at[0, 0:3], s_e.at[2])
    await_bytes(ey.at[0], s_e.at[3])


def write(tiles, row_t, weight, done, corr, hamil, late, mixed, sem):
    chunks, early = tiles.shape[0], done.shape[0]
    outs = (corr, hamil)

    def put(source, k):
        for a, out in enumerate(outs):
            columns = pl.ds(pl.multiple_of(k * LANES, LANES), LANES)
            keep(source.at[:, a * LANES : (a + 1) * LANES], out.at[:, columns], sem.at[a])

    pl.loop(0, early)(lambda k: put(done.at[k], k))

    @pl.loop(early, chunks)
    def _(k):
        def store(rows, value):
            late[k - early, rows, :] = value

        multiply(k, tiles, row_t, weight, mixed, store)
        put(late.at[k - early], k)

    for a, out in enumerate(outs):
        await_bytes(out, sem.at[a])


def body(derivs, grads, energies):
    chunks = 2048 // WIDTH
    early = chunks - TAIL
    quarter = chunks // 4

    def view(a):
        a = a.reshape(8, 2, 4, 4, 4, quarter, WIDTH).transpose(1, 2, 3, 4, 5, 0, 6)
        return pltpu.with_memory_space_constraint(a, pltpu.HBM)

    hbm = pl.BlockSpec(memory_space=pltpu.HBM)
    vmem = pl.BlockSpec(memory_space=pltpu.VMEM)
    dma = pltpu.SemaphoreType.DMA
    tiles, row_t, weight, done = pl.pallas_call(
        exchange,
        out_shape=(
            pltpu.VMEM((chunks, 2, 4, 4, 2, 4, 8, WIDTH), BF16),
            pltpu.VMEM((1024, 1024), BF16),
            pltpu.VMEM((1024, LANES), F32),
            pltpu.VMEM((early, 1024, 2 * WIDTH), F32),
        ),
        in_specs=[hbm, hbm, vmem],
        out_specs=(vmem,) * 4,
        scratch_shapes=[
            pltpu.VMEM((8, LANES), F32),
            pltpu.VMEM((chunks, 2, 4, 2, 4, 8, WIDTH), BF16),
            pltpu.VMEM((chunks, 2, 4, 2, 4, 8, WIDTH), BF16),
            pltpu.VMEM((2, 4, 2, quarter, 8, WIDTH), BF16),
            pltpu.VMEM((4, 4, 2, 4, quarter, 8, WIDTH), BF16),
            pltpu.VMEM((4, 4, 2, 4, quarter, 8, WIDTH), BF16),
            pltpu.VMEM((4, 8, LANES), F32),
            pltpu.VMEM((4, 4, 8, LANES), F32),
            pltpu.VMEM((2, 4, 4, 4, 8, LANES), F32),
            pltpu.VMEM((1024, 2 * WIDTH), BF16),
            dma, dma, dma, dma, dma((6,)), dma((4,)),
            dma((chunks,)), dma((chunks,)), dma((chunks,)), dma((chunks,)), dma((5,)), dma((4,)),
        ],
        compiler_params=pltpu.CompilerParams(
            collective_id=0, has_side_effects=True, vmem_limit_bytes=20 << 20
        ),
        name="exchange",
    )(view(derivs), view(grads), energies.reshape(1, 8))
    out = jax.ShapeDtypeStruct((1024, 2048), F32)
    return pl.pallas_call(
        write,
        out_shape=(out, out),
        in_specs=[vmem] * 4,
        out_specs=(hbm, hbm),
        scratch_shapes=[
            pltpu.VMEM((TAIL, 1024, 2 * WIDTH), F32),
            pltpu.VMEM((1024, 2 * WIDTH), BF16),
            dma((2,)),
        ],
        compiler_params=pltpu.CompilerParams(vmem_limit_bytes=8 << 20),
        name="write",
    )(tiles, row_t, weight, done)


def solution(mesh):
    placed = (P(("row", "col"), None), P(("row", "col"), None), P(("row", "col")))
    return jax.shard_map(
        body,
        mesh=mesh,
        in_specs=placed,
        out_specs=(P("row", "col"), P("row", "col")),
        check_vma=False,
    )
```

```python
import functools

import jax
import jax.numpy as jnp
from jax import lax
from jax.experimental import pallas as pl
from jax.experimental.pallas import tpu as pltpu
from jax.sharding import PartitionSpec as P

MESH = pl.DeviceIdType.MESH
LANES = 128
WIDTH = 128
EARLY_Z = 1
F_STEP = 3
F_LAG = 2
AT_ONCE = 2
AHEAD = 3
LAG_Y = 2
LAG_Z = 3
SLAB_STEP = 3
FIRST = 13
PIECES = 1
RELAY_LAG = 2
PACE = 3
BLOCK = 256
TAIL = 4
F32 = jnp.float32
BF16 = jnp.bfloat16


def place():
    row, col = lax.axis_index("row"), lax.axis_index("col")
    x, y = (col // 4) % 4, col % 4
    return x, y, (row // 2) * 2 + col // 16, row % 2


def device(x, y, z, core):
    return {"row": (z // 2) * 2 + core, "col": (z % 2) * 16 + x * 4 + y}


def send(src, dst, send_sem, recv_sem, target):
    pltpu.make_async_remote_copy(
        src, dst, send_sem, recv_sem, device_id=device(*target), device_id_type=MESH
    ).start()


def keep(src, dst, sem):
    pltpu.make_async_copy(src, dst, sem).start()


def await_bytes(ref, sem):
    pltpu.make_async_copy(ref, ref, sem).wait()


def multiply(k, tiles, row_t, weight, mixed, store):
    total = 1024
    width = tiles.shape[-1]
    sums = [jnp.zeros((8, width), F32)] * 2
    for i in range(8):
        sums = [
            s + tiles[k, i // 4, i % 4, :, a].astype(F32).reshape(16, 8, width).sum(axis=0)
            for a, s in enumerate(sums)
        ]
    means = [s.sum(axis=0, keepdims=True) / total for s in sums]
    for i in range(8):
        offset = tiles[k, i // 4, i % 4, :, 0].astype(F32).reshape(128, width) - means[0]
        grad = tiles[k, i // 4, i % 4, :, 1].astype(F32).reshape(128, width) - means[1]
        rows = slice(i * 128, (i + 1) * 128)
        mixed[rows, 0:width] = offset.astype(BF16)
        mixed[rows, width:] = (weight[rows, :] * offset + grad).astype(BF16)
    for i in range(total // BLOCK):
        rows = slice(i * BLOCK, (i + 1) * BLOCK)
        store(rows, jnp.dot(row_t[rows, :], mixed[...], preferred_element_type=F32) / total)


def exchange(
    derivs, grads, energies, tiles, row_t, weight, done,
    energy, zb, fb, xb, yb, r0, ra, rb, ez, ex, ey, mixed,
    s_f, s_x, s_y, s_z, s_c, s_r, s_e, fz_sem, fx_sem, slab_sem, x_sem, y_sem, z_sem, c_sem, r_sem, e_sem,
):
    x, y, z, core = place()
    chunks = tiles.shape[0]
    quarter = chunks // 4
    early = done.shape[0]
    mates = [(x, y, (z + d) % 4, core) for d in (2, 1, 3)]
    others = [(x, y, (z + d) % 4, 1 - core) for d in (0, 2, 1, 3)]
    along_x = [((x + d) % 4, y, z, core) for d in (2, 1, 3)]
    along_y = [(x, (y + d) % 4, z, core) for d in (2, 1, 3)]
    partner = (x, y, z, 1 - core)

    own = lax.broadcasted_iota(jnp.int32, (8, 8), 0) == lax.broadcasted_iota(jnp.int32, (8, 8), 1)
    column = jnp.where(own, energies[...], 0).sum(axis=1, keepdims=True)
    energy[0] = jnp.broadcast_to(column, (8, LANES))

    barrier = pltpu.get_barrier_semaphore()
    for peer in mates + others + along_x + along_y:
        pl.semaphore_signal(barrier, 1, device_id=device(*peer), device_id_type=MESH)
    pl.semaphore_wait(barrier, 13)

    @jax.named_scope("to_x")
    def to_x(k):
        for a, source in enumerate((derivs, grads)):
            for peer in along_x:
                block = source.at[:, peer[0], :, k // quarter, k % quarter]
                send(block, xb.at[k, :, :, a, x], s_x, x_sem.at[k], peer)
            block = source.at[:, x, :, k // quarter, k % quarter]
            keep(block, xb.at[k, :, :, a, x], x_sem.at[k])

    @jax.named_scope("to_y")
    def to_y(k):
        await_bytes(xb.at[k], x_sem.at[k])
        for peer in along_y:
            send(xb.at[k, :, peer[1]], yb.at[k, :, y], s_y, y_sem.at[k], peer)
        keep(xb.at[k, :, y], yb.at[k, :, y], y_sem.at[k])

    @jax.named_scope("to_z")
    def to_z(k):
        await_bytes(yb.at[k], y_sem.at[k])
        for peer in mates:
            send(yb.at[k, peer[2] % 2], tiles.at[k, core, z], s_z, z_sem.at[k], peer)
        keep(yb.at[k, z % 2], tiles.at[k, core, z], z_sem.at[k])

    @jax.named_scope("first_z")
    def first_z(k):
        for a, source in enumerate((derivs, grads)):
            for peer in mates:
                block = source.at[peer[2] % 2, :, :, k // quarter, k % quarter]
                send(block, zb.at[k, :, :, z, a], s_f.at[0], fz_sem.at[k], peer)
            block = source.at[z % 2, :, :, k // quarter, k % quarter]
            keep(block, zb.at[k, :, :, z, a], fz_sem.at[k])

    @jax.named_scope("first_x")
    def first_x(k):
        await_bytes(zb.at[k], fz_sem.at[k])
        for peer in along_x:
            send(zb.at[k, peer[0]], fb.at[k, :, :, :, x], s_f.at[1], fx_sem.at[k], peer)
        keep(zb.at[k, x], fb.at[k, :, :, :, x], fx_sem.at[k])

    @jax.named_scope("first_y")
    def first_y(k):
        await_bytes(fb.at[k], fx_sem.at[k])
        for peer in along_y:
            send(fb.at[k, peer[1]], tiles.at[k, core, :, y], s_f.at[2], z_sem.at[k], peer)
        keep(fb.at[k, y], tiles.at[k, core, :, y], z_sem.at[k])

    @jax.named_scope("to_partner")
    def to_partner(k):
        await_bytes(tiles.at[k, core], z_sem.at[k])
        send(tiles.at[k, core], tiles.at[k, core], s_c, c_sem.at[k], partner)

    @jax.named_scope("finish")
    def finish(k):
        await_bytes(tiles.at[k, 1 - core], c_sem.at[k])

        def store(rows, value):
            done[k, rows, :] = value

        multiply(k, tiles, row_t, weight, mixed, store)

    def when(condition, stage, k):
        pl.when(condition)(functools.partial(stage, k))

    @jax.named_scope("slab_direct")
    def slab_direct(piece):
        part = (slice(None), piece // 4, piece % 4)
        for peer in along_y[1:]:
            block = ra.at[(y, *part)]
            send(block, block, s_r.at[4], slab_sem.at[0, piece], peer)
        for peer in along_x[1:]:
            block = rb.at[(x, *part)]
            send(block, block, s_r.at[5], slab_sem.at[1, piece], peer)

    @jax.named_scope("slab_relay")
    def slab_relay(piece):
        part = (slice(None), piece // 4, piece % 4)
        back, ahead = 3 - 2 * (piece % 2), 1 + 2 * (piece % 2)
        await_bytes(ra.at[0:2, :, 0, 0], slab_sem.at[0, piece])
        block = ra.at[((y + back) % 4, *part)]
        send(block, block, s_r.at[6], r_sem.at[3], (x, (y + ahead) % 4, z, core))
        await_bytes(rb.at[0:2, :, 0, 0], slab_sem.at[1, piece])
        block = rb.at[((x + back) % 4, *part)]
        send(block, block, s_r.at[7], r_sem.at[4], ((x + ahead) % 4, y, z, core))

    rest = chunks - EARLY_Z

    def finished(i):
        return jnp.clip(jnp.minimum(PACE * (i + 1 - FIRST), i - LAG_Y - LAG_Z + EARLY_Z), 0, early)

    def step(i):
        when(i < rest, to_y, i + EARLY_Z)
        when(i + AHEAD < rest, to_x, i + AHEAD + EARLY_Z)
        when((i >= LAG_Y + 2) & (i < rest + LAG_Y), to_z, i - LAG_Y + EARLY_Z)
        late = i - LAG_Y - LAG_Z
        when((late >= 0) & (late < rest), to_partner, late + EARLY_Z)
        for j in range(PIECES):
            piece = (i - SLAB_STEP) * PIECES + j
            when((piece >= 0) & (piece < 8), slab_direct, piece)
            piece = piece - RELAY_LAG * PIECES
            when((piece >= 0) & (piece < 8), slab_relay, piece)
        first = i - F_STEP
        when((first >= 0) & (first < EARLY_Z), first_x, first)
        when((first >= F_LAG) & (first < EARLY_Z + F_LAG), first_y, first - F_LAG)
        when((first >= 2 * F_LAG) & (first < EARLY_Z + 2 * F_LAG), to_partner, first - 2 * F_LAG)

    lane = lax.broadcasted_iota(jnp.int32, (8, LANES), 1)

    def gather(blocks, stride):
        return sum(jnp.where((lane // stride) % 4 == i, blocks[i], 0) for i in range(4))

    to_x(EARLY_Z)
    for group, sem in ((mates, 0), (others, 1)):
        for peer in group:
            block = derivs.at[0, 0, peer[2] // 2, pl.ds(peer[3] * 2, 2)]
            send(block, r0.at[core, z], s_r.at[sem], r_sem.at[0], peer)
    keep(derivs.at[0, 0, z // 2, pl.ds(core * 2, 2)], r0.at[core, z], r_sem.at[0])
    for peer in mates:
        send(energy.at[0], ez.at[z], s_e.at[0], e_sem.at[0], peer)
    keep(energy.at[0], ez.at[z], e_sem.at[0])
    for k in range(EARLY_Z):
        first_z(k)
    pl.loop(EARLY_Z + 1, EARLY_Z + AT_ONCE)(to_x)
    to_y(EARLY_Z)

    with jax.named_scope("r1"):
        await_bytes(r0, r_sem.at[0])
        for peer in along_x:
            send(r0.at[:, :, 0], ra.at[y, x], s_r.at[2], r_sem.at[1], peer)
        keep(r0.at[:, :, 0], ra.at[y, x], r_sem.at[1])
        for peer in along_y:
            send(r0.at[:, :, 1], rb.at[x, y], s_r.at[3], r_sem.at[2], peer)
        keep(r0.at[:, :, 1], rb.at[x, y], r_sem.at[2])
    pl.loop(EARLY_Z + AT_ONCE, EARLY_Z + AHEAD + 1)(to_x)
    to_y(EARLY_Z + 1)
    to_x(EARLY_Z + AHEAD + 1)
    await_bytes(ez, e_sem.at[0])
    energy[1] = gather(ez, 32)
    to_z(EARLY_Z)
    to_y(EARLY_Z + 2)
    to_x(EARLY_Z + AHEAD + 2)
    to_z(EARLY_Z + 1)
    pl.loop(3, SLAB_STEP)(step)
    with jax.named_scope("r2"):
        for peer in along_x:
            send(energy.at[1], ex.at[x], s_e.at[1], e_sem.at[1], peer)
        keep(energy.at[1], ex.at[x], e_sem.at[1])
        await_bytes(ra.at[y], r_sem.at[1])
        await_bytes(rb.at[x], r_sem.at[2])

    middle = SLAB_STEP + 3
    pl.loop(SLAB_STEP, middle)(step)
    await_bytes(ex, e_sem.at[1])
    energy[2] = gather(ex, 8)
    step(middle)
    for peer in along_y:
        send(energy.at[2], ey.at[y], s_e.at[2], e_sem.at[2], peer)
    keep(energy.at[2], ey.at[y], e_sem.at[2])
    pl.loop(middle + 1, FIRST - 1)(step)
    with jax.named_scope("e"):
        await_bytes(ey, e_sem.at[2])
        energy[3] = gather(ey, 2)
    step(FIRST - 1)
    send(energy.at[3], energy.at[4], s_e.at[3], e_sem.at[3], partner)

    with jax.named_scope("r3"):
        await_bytes(ra.at[0], r_sem.at[3])
        await_bytes(rb.at[0], r_sem.at[4])

    @pl.loop(0, quarter)
    @jax.named_scope("prep")
    def _(c):
        for half, source in enumerate((ra, rb)):
            blocks = []
            for i in range(8):
                block = source[:, :, i // 4, i % 4, c].astype(F32)
                if half == 1:
                    block = jnp.stack([block[:, j] for j in range(4)])
                blocks.append(block.reshape(128, LANES))
            total = sum(b.reshape(16, 8, LANES).sum(axis=0) for b in blocks)
            mean = total.sum(axis=0, keepdims=True) / 1024
            rows = pl.ds(pl.multiple_of((half * quarter + c) * LANES, LANES), LANES)
            for i, block in enumerate(blocks):
                row_t[rows, i * 128 : (i + 1) * 128] = (block - mean).T.astype(BF16)

    with jax.named_scope("w"):
        await_bytes(energy.at[4], e_sem.at[3])
        every = jnp.where(lane % 2 == core, energy[3], energy[4])
        every = every - every.sum(axis=0, keepdims=True).sum(axis=1, keepdims=True) / 1024
        for i in range(128):
            at = (i // 16 % 4) * 32 + (i % 4) * 8 + (i // 4 % 4) * 2 + i // 64
            weight[i * 8 : i * 8 + 8, :] = jnp.broadcast_to(every[:, at : at + 1], (8, LANES))

    @pl.loop(FIRST, rest + LAG_Y + LAG_Z)
    def _(i):
        step(i)
        pl.loop(finished(i - 1), finished(i))(finish)

    pl.loop(finished(chunks + LAG_Y + LAG_Z - 1), early)(finish)
    pl.loop(early, chunks)(lambda k: await_bytes(tiles.at[k, 1 - core], c_sem.at[k]))

    await_bytes(zb.at[:, 0:3], s_f.at[0])
    await_bytes(fb.at[:, 0:3], s_f.at[1])
    await_bytes(fb.at[:, 0:3], s_f.at[2])
    await_bytes(xb.at[EARLY_Z:, :, 0:3], s_x)
    await_bytes(yb.at[EARLY_Z:, :, 0:3], s_y)
    await_bytes(tiles.at[EARLY_Z:, 0, 0:3], s_z)
    await_bytes(tiles.at[:, 0], s_c)
    await_bytes(r0.at[0, 0:3], s_r.at[0])
    await_bytes(r0.at[0], s_r.at[1])
    await_bytes(ra.at[0, 0:3], s_r.at[2])
    await_bytes(rb.at[0, 0:3], s_r.at[3])
    await_bytes(ra.at[0:2], s_r.at[4])
    await_bytes(rb.at[0:2], s_r.at[5])
    await_bytes(ra.at[0], s_r.at[6])
    await_bytes(rb.at[0], s_r.at[7])
    await_bytes(ez.at[0:3], s_e.at[0])
    await_bytes(ex.at[0:3], s_e.at[1])
    await_bytes(ey.at[0:3], s_e.at[2])
    await_bytes(energy.at[3], s_e.at[3])


def write(tiles, row_t, weight, done, corr, hamil, late, mixed, sem):
    chunks, early = tiles.shape[0], done.shape[0]
    outs = (corr, hamil)

    def put(source, k):
        for a, out in enumerate(outs):
            columns = pl.ds(pl.multiple_of(k * LANES, LANES), LANES)
            keep(source.at[:, a * LANES : (a + 1) * LANES], out.at[:, columns], sem.at[a])

    pl.loop(0, early)(lambda k: put(done.at[k], k))

    @pl.loop(early, chunks)
    def _(k):
        def store(rows, value):
            late[k - early, rows, :] = value

        multiply(k, tiles, row_t, weight, mixed, store)
        put(late.at[k - early], k)

    for a, out in enumerate(outs):
        await_bytes(out, sem.at[a])


def body(derivs, grads, energies):
    chunks = 2048 // WIDTH
    early = chunks - TAIL
    quarter = chunks // 4

    def view(a):
        a = a.reshape(8, 2, 4, 4, 4, quarter, WIDTH).transpose(1, 2, 3, 4, 5, 0, 6)
        return pltpu.with_memory_space_constraint(a, pltpu.HBM)

    hbm = pl.BlockSpec(memory_space=pltpu.HBM)
    vmem = pl.BlockSpec(memory_space=pltpu.VMEM)
    dma = pltpu.SemaphoreType.DMA
    tiles, row_t, weight, done = pl.pallas_call(
        exchange,
        out_shape=(
            pltpu.VMEM((chunks, 2, 4, 4, 2, 4, 8, WIDTH), BF16),
            pltpu.VMEM((1024, 1024), BF16),
            pltpu.VMEM((1024, LANES), F32),
            pltpu.VMEM((early, 1024, 2 * WIDTH), F32),
        ),
        in_specs=[hbm, hbm, vmem],
        out_specs=(vmem,) * 4,
        scratch_shapes=[
            pltpu.VMEM((5, 8, LANES), F32),
            pltpu.VMEM((EARLY_Z, 4, 4, 4, 2, 8, WIDTH), BF16),
            pltpu.VMEM((EARLY_Z, 4, 4, 2, 4, 8, WIDTH), BF16),
            pltpu.VMEM((chunks, 2, 4, 2, 4, 8, WIDTH), BF16),
            pltpu.VMEM((chunks, 2, 4, 2, 4, 8, WIDTH), BF16),
            pltpu.VMEM((2, 4, 2, quarter, 8, WIDTH), BF16),
            pltpu.VMEM((4, 4, 2, 4, quarter, 8, WIDTH), BF16),
            pltpu.VMEM((4, 4, 2, 4, quarter, 8, WIDTH), BF16),
            pltpu.VMEM((4, 8, LANES), F32),
            pltpu.VMEM((4, 8, LANES), F32),
            pltpu.VMEM((4, 8, LANES), F32),
            pltpu.VMEM((1024, 2 * WIDTH), BF16),
            dma((3,)), dma, dma, dma, dma, dma((8,)), dma((4,)), dma((EARLY_Z,)), dma((EARLY_Z,)), dma((2, 8)),
            dma((chunks,)), dma((chunks,)), dma((chunks,)), dma((chunks,)), dma((5,)), dma((4,)),
        ],
        compiler_params=pltpu.CompilerParams(
            collective_id=0, has_side_effects=True, vmem_limit_bytes=20 << 20
        ),
        name="exchange",
    )(view(derivs), view(grads), energies.reshape(1, 8))
    out = jax.ShapeDtypeStruct((1024, 2048), F32)
    return pl.pallas_call(
        write,
        out_shape=(out, out),
        in_specs=[vmem] * 4,
        out_specs=(hbm, hbm),
        scratch_shapes=[
            pltpu.VMEM((TAIL, 1024, 2 * WIDTH), F32),
            pltpu.VMEM((1024, 2 * WIDTH), BF16),
            dma((2,)),
        ],
        compiler_params=pltpu.CompilerParams(vmem_limit_bytes=8 << 20),
        name="write",
    )(tiles, row_t, weight, done)


def solution(mesh):
    placed = (P(("row", "col"), None), P(("row", "col"), None), P(("row", "col")))
    return jax.shard_map(
        body,
        mesh=mesh,
        in_specs=placed,
        out_specs=(P("row", "col"), P("row", "col")),
        check_vma=False,
    )
```

```python
import functools

import jax
import jax.numpy as jnp
from jax import lax
from jax.experimental import pallas as pl
from jax.experimental.pallas import tpu as pltpu
from jax.sharding import PartitionSpec as P

MESH = pl.DeviceIdType.MESH
LANES = 128
WIDTH = 128
EARLY_Z = 2
F_STEP = 6
F_LAG = 3
AT_ONCE = 2
AHEAD = 3
LAG_Y = 2
LAG_Z = 3
SLAB_FIRST = 2
FIRST = 12
RELAY_LAG = 3
PACE = 3
BLOCK = 256
TAIL = 4
F32 = jnp.float32
BF16 = jnp.bfloat16


def place():
    row, col = lax.axis_index("row"), lax.axis_index("col")
    x, y = (col // 4) % 4, col % 4
    return x, y, (row // 2) * 2 + col // 16, row % 2


def device(x, y, z, core):
    return {"row": (z // 2) * 2 + core, "col": (z % 2) * 16 + x * 4 + y}


def send(src, dst, send_sem, recv_sem, target):
    pltpu.make_async_remote_copy(
        src, dst, send_sem, recv_sem, device_id=device(*target), device_id_type=MESH
    ).start()


def keep(src, dst, sem):
    pltpu.make_async_copy(src, dst, sem).start()


def await_bytes(ref, sem):
    pltpu.make_async_copy(ref, ref, sem).wait()


def multiply(k, tiles, row_t, weight, mixed, store):
    total = 1024
    width = tiles.shape[-1]
    sums = [jnp.zeros((8, width), F32)] * 2
    for i in range(8):
        sums = [
            s + tiles[k, i // 4, i % 4, :, a].astype(F32).reshape(16, 8, width).sum(axis=0)
            for a, s in enumerate(sums)
        ]
    means = [s.sum(axis=0, keepdims=True) / total for s in sums]
    for i in range(8):
        offset = tiles[k, i // 4, i % 4, :, 0].astype(F32).reshape(128, width) - means[0]
        grad = tiles[k, i // 4, i % 4, :, 1].astype(F32).reshape(128, width) - means[1]
        rows = slice(i * 128, (i + 1) * 128)
        mixed[rows, 0:width] = offset.astype(BF16)
        mixed[rows, width:] = (weight[rows, :] * offset + grad).astype(BF16)
    for i in range(total // BLOCK):
        rows = slice(i * BLOCK, (i + 1) * BLOCK)
        store(rows, jnp.dot(row_t[rows, :], mixed[...], preferred_element_type=F32) / total)


def exchange(
    derivs, grads, energies, tiles, row_t, weight, done,
    energy, zb, fb, xb, yb, r0, ra, rb, ez, ex, ey, mixed,
    s_f, s_x, s_y, s_z, s_c, s_r, s_e, fz_sem, fx_sem, slab_sem, x_sem, y_sem, z_sem, c_sem, r_sem, e_sem,
):
    x, y, z, core = place()
    chunks = tiles.shape[0]
    quarter = chunks // 4
    early = done.shape[0]
    mates = [(x, y, (z + d) % 4, core) for d in (2, 1, 3)]
    others = [(x, y, (z + d) % 4, 1 - core) for d in (0, 2, 1, 3)]
    along_x = [((x + d) % 4, y, z, core) for d in (2, 1, 3)]
    along_y = [(x, (y + d) % 4, z, core) for d in (2, 1, 3)]
    partner = (x, y, z, 1 - core)

    own = lax.broadcasted_iota(jnp.int32, (8, 8), 0) == lax.broadcasted_iota(jnp.int32, (8, 8), 1)
    column = jnp.where(own, energies[...], 0).sum(axis=1, keepdims=True)
    energy[0] = jnp.broadcast_to(column, (8, LANES))

    barrier = pltpu.get_barrier_semaphore()
    for peer in mates + others + along_x + along_y:
        pl.semaphore_signal(barrier, 1, device_id=device(*peer), device_id_type=MESH)
    pl.semaphore_wait(barrier, 13)

    @jax.named_scope("to_x")
    def to_x(k):
        for a, source in enumerate((derivs, grads)):
            for peer in along_x:
                block = source.at[:, peer[0], :, k // quarter, k % quarter]
                send(block, xb.at[k, :, :, a, x], s_x, x_sem.at[k], peer)
            block = source.at[:, x, :, k // quarter, k % quarter]
            keep(block, xb.at[k, :, :, a, x], x_sem.at[k])

    @jax.named_scope("to_y")
    def to_y(k):
        await_bytes(xb.at[k], x_sem.at[k])
        for peer in along_y:
            send(xb.at[k, :, peer[1]], yb.at[k, :, y], s_y, y_sem.at[k], peer)
        keep(xb.at[k, :, y], yb.at[k, :, y], y_sem.at[k])

    @jax.named_scope("to_z")
    def to_z(k):
        await_bytes(yb.at[k], y_sem.at[k])
        for peer in mates:
            send(yb.at[k, peer[2] % 2], tiles.at[k, core, z], s_z, z_sem.at[k], peer)
        keep(yb.at[k, z % 2], tiles.at[k, core, z], z_sem.at[k])

    @jax.named_scope("first_z")
    def first_z(k):
        for a, source in enumerate((derivs, grads)):
            for peer in mates:
                block = source.at[peer[2] % 2, :, :, k // quarter, k % quarter]
                send(block, zb.at[k, :, :, z, a], s_f.at[0], fz_sem.at[k], peer)
            block = source.at[z % 2, :, :, k // quarter, k % quarter]
            keep(block, zb.at[k, :, :, z, a], fz_sem.at[k])

    @jax.named_scope("first_x")
    def first_x(k):
        await_bytes(zb.at[k], fz_sem.at[k])
        for peer in along_x:
            send(zb.at[k, peer[0]], fb.at[k, :, :, :, x], s_f.at[1], fx_sem.at[k], peer)
        keep(zb.at[k, x], fb.at[k, :, :, :, x], fx_sem.at[k])

    @jax.named_scope("first_y")
    def first_y(k):
        await_bytes(fb.at[k], fx_sem.at[k])
        for peer in along_y:
            send(fb.at[k, peer[1]], tiles.at[k, core, :, y], s_f.at[2], z_sem.at[k], peer)
        keep(fb.at[k, y], tiles.at[k, core, :, y], z_sem.at[k])

    @jax.named_scope("to_partner")
    def to_partner(k):
        await_bytes(tiles.at[k, core], z_sem.at[k])
        send(tiles.at[k, core], tiles.at[k, core], s_c, c_sem.at[k], partner)

    @jax.named_scope("finish")
    def finish(j):
        turn = early - EARLY_Z
        k = jnp.where(j < turn, j + EARLY_Z, j - turn)
        await_bytes(tiles.at[k, 1 - core], c_sem.at[k])

        def store(rows, value):
            done[k, rows, :] = value

        multiply(k, tiles, row_t, weight, mixed, store)

    def when(condition, stage, k):
        pl.when(condition)(functools.partial(stage, k))

    @jax.named_scope("slab_direct")
    def slab_direct(piece):
        part = (slice(None), piece // 4, piece % 4)
        for peer in along_y[1:]:
            block = ra.at[(y, *part)]
            send(block, block, s_r.at[4], slab_sem.at[0, piece], peer)
        for peer in along_x[1:]:
            block = rb.at[(x, *part)]
            send(block, block, s_r.at[5], slab_sem.at[1, piece], peer)

    @jax.named_scope("slab_relay")
    def slab_relay(piece):
        part = (slice(None), piece // 4, piece % 4)
        back, ahead = 3 - 2 * (piece % 2), 1 + 2 * (piece % 2)
        await_bytes(ra.at[0:2, :, 0, 0], slab_sem.at[0, piece])
        block = ra.at[((y + back) % 4, *part)]
        send(block, block, s_r.at[6], r_sem.at[3], (x, (y + ahead) % 4, z, core))
        await_bytes(rb.at[0:2, :, 0, 0], slab_sem.at[1, piece])
        block = rb.at[((x + back) % 4, *part)]
        send(block, block, s_r.at[7], r_sem.at[4], ((x + ahead) % 4, y, z, core))

    rest = chunks - EARLY_Z

    def finished(i):
        return jnp.clip(jnp.minimum(PACE * (i + 1 - FIRST), i - LAG_Y - LAG_Z), 0, early)

    def step(i):
        when(i < rest, to_y, i + EARLY_Z)
        when(i + AHEAD < rest, to_x, i + AHEAD + EARLY_Z)
        when((i >= LAG_Y + 2) & (i < rest + LAG_Y), to_z, i - LAG_Y + EARLY_Z)
        late = i - LAG_Y - LAG_Z
        when((late >= 0) & (late < rest), to_partner, late + EARLY_Z)
        piece = i - 2 + SLAB_FIRST
        when(piece < 8, slab_direct, piece)
        piece = piece - RELAY_LAG
        when((piece >= 0) & (piece < 8), slab_relay, piece)
        first = i - F_STEP
        when((first >= 0) & (first < EARLY_Z), first_x, first)
        when((first >= F_LAG) & (first < EARLY_Z + F_LAG), first_y, first - F_LAG)
        when((first >= 2 * F_LAG) & (first < EARLY_Z + 2 * F_LAG), to_partner, first - 2 * F_LAG)

    lane = lax.broadcasted_iota(jnp.int32, (8, LANES), 1)

    def gather(blocks, stride):
        return sum(jnp.where((lane // stride) % 4 == i, blocks[i], 0) for i in range(4))

    to_x(EARLY_Z)
    for group, sem in ((mates, 0), (others, 1)):
        for peer in group:
            block = derivs.at[0, 0, peer[2] // 2, pl.ds(peer[3] * 2, 2)]
            send(block, r0.at[core, z], s_r.at[sem], r_sem.at[0], peer)
    keep(derivs.at[0, 0, z // 2, pl.ds(core * 2, 2)], r0.at[core, z], r_sem.at[0])
    for peer in mates:
        send(energy.at[0], ez.at[z], s_e.at[0], e_sem.at[0], peer)
    keep(energy.at[0], ez.at[z], e_sem.at[0])
    for k in range(EARLY_Z):
        first_z(k)
    pl.loop(EARLY_Z + 1, EARLY_Z + AT_ONCE)(to_x)
    to_y(EARLY_Z)

    with jax.named_scope("r1"):
        await_bytes(r0, r_sem.at[0])
        for peer in along_x:
            send(r0.at[:, :, 0], ra.at[y, x], s_r.at[2], r_sem.at[1], peer)
        keep(r0.at[:, :, 0], ra.at[y, x], r_sem.at[1])
        for peer in along_y:
            send(r0.at[:, :, 1], rb.at[x, y], s_r.at[3], r_sem.at[2], peer)
        keep(r0.at[:, :, 1], rb.at[x, y], r_sem.at[2])
    pl.loop(EARLY_Z + AT_ONCE, EARLY_Z + AHEAD + 1)(to_x)
    to_y(EARLY_Z + 1)
    to_x(EARLY_Z + AHEAD + 1)
    await_bytes(ez, e_sem.at[0])
    energy[1] = gather(ez, 32)
    to_z(EARLY_Z)
    with jax.named_scope("r2"):
        await_bytes(ra.at[y], r_sem.at[1])
        await_bytes(rb.at[x], r_sem.at[2])
        for piece in range(SLAB_FIRST):
            slab_direct(piece)
    to_y(EARLY_Z + 2)
    to_x(EARLY_Z + AHEAD + 2)
    to_z(EARLY_Z + 1)
    slab_direct(SLAB_FIRST)
    for peer in along_x:
        send(energy.at[1], ex.at[x], s_e.at[1], e_sem.at[1], peer)
    keep(energy.at[1], ex.at[x], e_sem.at[1])
    middle = 6
    pl.loop(3, middle)(step)
    await_bytes(ex, e_sem.at[1])
    energy[2] = gather(ex, 8)
    step(middle)
    for peer in along_y:
        send(energy.at[2], ey.at[y], s_e.at[2], e_sem.at[2], peer)
    keep(energy.at[2], ey.at[y], e_sem.at[2])
    pl.loop(middle + 1, FIRST - 1)(step)
    with jax.named_scope("e"):
        await_bytes(ey, e_sem.at[2])
        energy[3] = gather(ey, 2)
    step(FIRST - 1)
    send(energy.at[3], energy.at[4], s_e.at[3], e_sem.at[3], partner)

    with jax.named_scope("r3"):
        await_bytes(ra.at[0], r_sem.at[3])
        await_bytes(rb.at[0], r_sem.at[4])

    @pl.loop(0, quarter)
    @jax.named_scope("prep")
    def _(c):
        for half, source in enumerate((ra, rb)):
            blocks = []
            for i in range(8):
                block = source[:, :, i // 4, i % 4, c].astype(F32)
                if half == 1:
                    block = jnp.stack([block[:, j] for j in range(4)])
                blocks.append(block.reshape(128, LANES))
            total = sum(b.reshape(16, 8, LANES).sum(axis=0) for b in blocks)
            mean = total.sum(axis=0, keepdims=True) / 1024
            rows = pl.ds(pl.multiple_of((half * quarter + c) * LANES, LANES), LANES)
            for i, block in enumerate(blocks):
                row_t[rows, i * 128 : (i + 1) * 128] = (block - mean).T.astype(BF16)

    with jax.named_scope("w"):
        await_bytes(energy.at[4], e_sem.at[3])
        every = jnp.where(lane % 2 == core, energy[3], energy[4])
        every = every - every.sum(axis=0, keepdims=True).sum(axis=1, keepdims=True) / 1024
        for i in range(128):
            at = (i // 16 % 4) * 32 + (i % 4) * 8 + (i // 4 % 4) * 2 + i // 64
            weight[i * 8 : i * 8 + 8, :] = jnp.broadcast_to(every[:, at : at + 1], (8, LANES))

    @pl.loop(FIRST, rest + LAG_Y + LAG_Z)
    def _(i):
        step(i)
        pl.loop(finished(i - 1), finished(i))(finish)

    pl.loop(finished(chunks + LAG_Y + LAG_Z - 1), early)(finish)
    pl.loop(early, chunks)(lambda k: await_bytes(tiles.at[k, 1 - core], c_sem.at[k]))

    await_bytes(zb.at[:, 0:3], s_f.at[0])
    await_bytes(fb.at[:, 0:3], s_f.at[1])
    await_bytes(fb.at[:, 0:3], s_f.at[2])
    await_bytes(xb.at[EARLY_Z:, :, 0:3], s_x)
    await_bytes(yb.at[EARLY_Z:, :, 0:3], s_y)
    await_bytes(tiles.at[EARLY_Z:, 0, 0:3], s_z)
    await_bytes(tiles.at[:, 0], s_c)
    await_bytes(r0.at[0, 0:3], s_r.at[0])
    await_bytes(r0.at[0], s_r.at[1])
    await_bytes(ra.at[0, 0:3], s_r.at[2])
    await_bytes(rb.at[0, 0:3], s_r.at[3])
    await_bytes(ra.at[0:2], s_r.at[4])
    await_bytes(rb.at[0:2], s_r.at[5])
    await_bytes(ra.at[0], s_r.at[6])
    await_bytes(rb.at[0], s_r.at[7])
    await_bytes(ez.at[0:3], s_e.at[0])
    await_bytes(ex.at[0:3], s_e.at[1])
    await_bytes(ey.at[0:3], s_e.at[2])
    await_bytes(energy.at[3], s_e.at[3])


def write(tiles, row_t, weight, done, corr, hamil, late, mixed, sem):
    chunks, early = tiles.shape[0], done.shape[0]
    outs = (corr, hamil)

    def put(source, k):
        for a, out in enumerate(outs):
            columns = pl.ds(pl.multiple_of(k * LANES, LANES), LANES)
            keep(source.at[:, a * LANES : (a + 1) * LANES], out.at[:, columns], sem.at[a])

    pl.loop(0, early)(lambda k: put(done.at[k], k))

    @pl.loop(early, chunks)
    def _(k):
        def store(rows, value):
            late[k - early, rows, :] = value

        multiply(k, tiles, row_t, weight, mixed, store)
        put(late.at[k - early], k)

    for a, out in enumerate(outs):
        await_bytes(out, sem.at[a])


def body(derivs, grads, energies):
    chunks = 2048 // WIDTH
    early = chunks - TAIL
    quarter = chunks // 4

    def view(a):
        a = a.reshape(8, 2, 4, 4, 4, quarter, WIDTH).transpose(1, 2, 3, 4, 5, 0, 6)
        return pltpu.with_memory_space_constraint(a, pltpu.HBM)

    hbm = pl.BlockSpec(memory_space=pltpu.HBM)
    vmem = pl.BlockSpec(memory_space=pltpu.VMEM)
    dma = pltpu.SemaphoreType.DMA
    tiles, row_t, weight, done = pl.pallas_call(
        exchange,
        out_shape=(
            pltpu.VMEM((chunks, 2, 4, 4, 2, 4, 8, WIDTH), BF16),
            pltpu.VMEM((1024, 1024), BF16),
            pltpu.VMEM((1024, LANES), F32),
            pltpu.VMEM((early, 1024, 2 * WIDTH), F32),
        ),
        in_specs=[hbm, hbm, vmem],
        out_specs=(vmem,) * 4,
        scratch_shapes=[
            pltpu.VMEM((5, 8, LANES), F32),
            pltpu.VMEM((EARLY_Z, 4, 4, 4, 2, 8, WIDTH), BF16),
            pltpu.VMEM((EARLY_Z, 4, 4, 2, 4, 8, WIDTH), BF16),
            pltpu.VMEM((chunks, 2, 4, 2, 4, 8, WIDTH), BF16),
            pltpu.VMEM((chunks, 2, 4, 2, 4, 8, WIDTH), BF16),
            pltpu.VMEM((2, 4, 2, quarter, 8, WIDTH), BF16),
            pltpu.VMEM((4, 4, 2, 4, quarter, 8, WIDTH), BF16),
            pltpu.VMEM((4, 4, 2, 4, quarter, 8, WIDTH), BF16),
            pltpu.VMEM((4, 8, LANES), F32),
            pltpu.VMEM((4, 8, LANES), F32),
            pltpu.VMEM((4, 8, LANES), F32),
            pltpu.VMEM((1024, 2 * WIDTH), BF16),
            dma((3,)), dma, dma, dma, dma, dma((8,)), dma((4,)), dma((EARLY_Z,)), dma((EARLY_Z,)), dma((2, 8)),
            dma((chunks,)), dma((chunks,)), dma((chunks,)), dma((chunks,)), dma((5,)), dma((4,)),
        ],
        compiler_params=pltpu.CompilerParams(
            collective_id=0, has_side_effects=True, vmem_limit_bytes=20 << 20
        ),
        name="exchange",
    )(view(derivs), view(grads), energies.reshape(1, 8))
    out = jax.ShapeDtypeStruct((1024, 2048), F32)
    return pl.pallas_call(
        write,
        out_shape=(out, out),
        in_specs=[vmem] * 4,
        out_specs=(hbm, hbm),
        scratch_shapes=[
            pltpu.VMEM((TAIL, 1024, 2 * WIDTH), F32),
            pltpu.VMEM((1024, 2 * WIDTH), BF16),
            dma((2,)),
        ],
        compiler_params=pltpu.CompilerParams(vmem_limit_bytes=8 << 20),
        name="write",
    )(tiles, row_t, weight, done)


def solution(mesh):
    placed = (P(("row", "col"), None), P(("row", "col"), None), P(("row", "col")))
    return jax.shard_map(
        body,
        mesh=mesh,
        in_specs=placed,
        out_specs=(P("row", "col"), P("row", "col")),
        check_vma=False,
    )
```

```python
import functools

import jax
import jax.numpy as jnp
from jax import lax
from jax.experimental import pallas as pl
from jax.experimental.pallas import tpu as pltpu
from jax.sharding import PartitionSpec as P

MESH = pl.DeviceIdType.MESH
LANES = 128
WIDTH = 128
EARLY_Z = 2
F_STEP = 6
F_LAG = 3
AT_ONCE = 2
AHEAD = 3
LAG_Y = 2
LAG_Z = 4
SLAB_FIRST = 2
FIRST = 12
RELAY_LAG = 3
PACE = 3
BLOCK = 256
TAIL = 4
F32 = jnp.float32
BF16 = jnp.bfloat16


def place():
    row, col = lax.axis_index("row"), lax.axis_index("col")
    x, y = (col // 4) % 4, col % 4
    return x, y, (row // 2) * 2 + col // 16, row % 2


def device(x, y, z, core):
    return {"row": (z // 2) * 2 + core, "col": (z % 2) * 16 + x * 4 + y}


def send(src, dst, send_sem, recv_sem, target):
    pltpu.make_async_remote_copy(
        src, dst, send_sem, recv_sem, device_id=device(*target), device_id_type=MESH
    ).start()


def keep(src, dst, sem):
    pltpu.make_async_copy(src, dst, sem).start()


def await_bytes(ref, sem):
    pltpu.make_async_copy(ref, ref, sem).wait()


def multiply(k, tiles, row_t, weight, mixed, store):
    total = 1024
    width = tiles.shape[-1]
    sums = [jnp.zeros((8, width), F32)] * 2
    for i in range(8):
        sums = [
            s + tiles[k, i // 4, i % 4, :, a].astype(F32).reshape(16, 8, width).sum(axis=0)
            for a, s in enumerate(sums)
        ]
    means = [s.sum(axis=0, keepdims=True) / total for s in sums]
    for i in range(8):
        offset = tiles[k, i // 4, i % 4, :, 0].astype(F32).reshape(128, width) - means[0]
        grad = tiles[k, i // 4, i % 4, :, 1].astype(F32).reshape(128, width) - means[1]
        rows = slice(i * 128, (i + 1) * 128)
        mixed[rows, 0:width] = offset.astype(BF16)
        mixed[rows, width:] = (weight[rows, :] * offset + grad).astype(BF16)
    for i in range(total // BLOCK):
        rows = slice(i * BLOCK, (i + 1) * BLOCK)
        store(rows, jnp.dot(row_t[rows, :], mixed[...], preferred_element_type=F32) / total)


def exchange(
    derivs, grads, energies, tiles, row_t, weight, done,
    energy, zb, fb, xb, yb, r0, ra, rb, ez, ex, ey, mixed,
    s_f, s_x, s_y, s_z, s_c, s_r, s_e, fz_sem, fx_sem, slab_sem, x_sem, y_sem, z_sem, c_sem, r_sem, e_sem,
):
    x, y, z, core = place()
    chunks = tiles.shape[0]
    quarter = chunks // 4
    early = done.shape[0]
    mates = [(x, y, (z + d) % 4, core) for d in (2, 1, 3)]
    others = [(x, y, (z + d) % 4, 1 - core) for d in (0, 2, 1, 3)]
    along_x = [((x + d) % 4, y, z, core) for d in (2, 1, 3)]
    along_y = [(x, (y + d) % 4, z, core) for d in (2, 1, 3)]
    partner = (x, y, z, 1 - core)

    own = lax.broadcasted_iota(jnp.int32, (8, 8), 0) == lax.broadcasted_iota(jnp.int32, (8, 8), 1)
    column = jnp.where(own, energies[...], 0).sum(axis=1, keepdims=True)
    energy[0] = jnp.broadcast_to(column, (8, LANES))

    barrier = pltpu.get_barrier_semaphore()
    for peer in mates + others + along_x + along_y:
        pl.semaphore_signal(barrier, 1, device_id=device(*peer), device_id_type=MESH)
    pl.semaphore_wait(barrier, 13)

    @jax.named_scope("to_x")
    def to_x(k):
        for a, source in enumerate((derivs, grads)):
            for peer in along_x:
                block = source.at[:, peer[0], :, k // quarter, k % quarter]
                send(block, xb.at[k, :, :, a, x], s_x, x_sem.at[k], peer)
            block = source.at[:, x, :, k // quarter, k % quarter]
            keep(block, xb.at[k, :, :, a, x], x_sem.at[k])

    @jax.named_scope("to_y")
    def to_y(k):
        await_bytes(xb.at[k], x_sem.at[k])
        for peer in along_y:
            send(xb.at[k, :, peer[1]], yb.at[k, :, y], s_y, y_sem.at[k], peer)
        keep(xb.at[k, :, y], yb.at[k, :, y], y_sem.at[k])

    @jax.named_scope("to_z")
    def to_z(k):
        await_bytes(yb.at[k], y_sem.at[k])
        for peer in mates:
            send(yb.at[k, peer[2] % 2], tiles.at[k, core, z], s_z, z_sem.at[k], peer)
        keep(yb.at[k, z % 2], tiles.at[k, core, z], z_sem.at[k])

    @jax.named_scope("first_z")
    def first_z(k):
        for a, source in enumerate((derivs, grads)):
            for peer in mates:
                block = source.at[peer[2] % 2, :, :, k // quarter, k % quarter]
                send(block, zb.at[k, :, :, z, a], s_f.at[0], fz_sem.at[k], peer)
            block = source.at[z % 2, :, :, k // quarter, k % quarter]
            keep(block, zb.at[k, :, :, z, a], fz_sem.at[k])

    @jax.named_scope("first_x")
    def first_x(k):
        await_bytes(zb.at[k], fz_sem.at[k])
        for peer in along_x:
            send(zb.at[k, peer[0]], fb.at[k, :, :, :, x], s_f.at[1], fx_sem.at[k], peer)
        keep(zb.at[k, x], fb.at[k, :, :, :, x], fx_sem.at[k])

    @jax.named_scope("first_y")
    def first_y(k):
        await_bytes(fb.at[k], fx_sem.at[k])
        for peer in along_y:
            send(fb.at[k, peer[1]], tiles.at[k, core, :, y], s_f.at[2], z_sem.at[k], peer)
        keep(fb.at[k, y], tiles.at[k, core, :, y], z_sem.at[k])

    @jax.named_scope("to_partner")
    def to_partner(k):
        await_bytes(tiles.at[k, core], z_sem.at[k])
        send(tiles.at[k, core], tiles.at[k, core], s_c, c_sem.at[k], partner)

    @jax.named_scope("finish")
    def finish(j):
        turn = early - EARLY_Z
        k = jnp.where(j < turn, j + EARLY_Z, j - turn)
        await_bytes(tiles.at[k, 1 - core], c_sem.at[k])

        def store(rows, value):
            done[k, rows, :] = value

        multiply(k, tiles, row_t, weight, mixed, store)

    def when(condition, stage, k):
        pl.when(condition)(functools.partial(stage, k))

    @jax.named_scope("slab_direct")
    def slab_direct(piece):
        part = (slice(None), piece // 4, piece % 4)
        for peer in along_y[1:]:
            block = ra.at[(y, *part)]
            send(block, block, s_r.at[4], slab_sem.at[0, piece], peer)
        for peer in along_x[1:]:
            block = rb.at[(x, *part)]
            send(block, block, s_r.at[5], slab_sem.at[1, piece], peer)

    @jax.named_scope("slab_relay")
    def slab_relay(piece):
        part = (slice(None), piece // 4, piece % 4)
        back, ahead = 3 - 2 * (piece % 2), 1 + 2 * (piece % 2)
        await_bytes(ra.at[0:2, :, 0, 0], slab_sem.at[0, piece])
        block = ra.at[((y + back) % 4, *part)]
        send(block, block, s_r.at[6], r_sem.at[3], (x, (y + ahead) % 4, z, core))
        await_bytes(rb.at[0:2, :, 0, 0], slab_sem.at[1, piece])
        block = rb.at[((x + back) % 4, *part)]
        send(block, block, s_r.at[7], r_sem.at[4], ((x + ahead) % 4, y, z, core))

    rest = chunks - EARLY_Z

    def finished(i):
        return jnp.clip(jnp.minimum(PACE * (i + 1 - FIRST), i - LAG_Y - LAG_Z), 0, early)

    def step(i):
        when(i < rest, to_y, i + EARLY_Z)
        when(i + AHEAD < rest, to_x, i + AHEAD + EARLY_Z)
        when((i >= LAG_Y + 2) & (i < rest + LAG_Y), to_z, i - LAG_Y + EARLY_Z)
        late = i - LAG_Y - LAG_Z
        when((late >= 0) & (late < rest), to_partner, late + EARLY_Z)
        piece = i - 2 + SLAB_FIRST
        when(piece < 8, slab_direct, piece)
        piece = piece - RELAY_LAG
        when((piece >= 0) & (piece < 8), slab_relay, piece)
        first = i - F_STEP
        when((first >= 0) & (first < EARLY_Z), first_x, first)
        when((first >= F_LAG) & (first < EARLY_Z + F_LAG), first_y, first - F_LAG)
        when((first >= 2 * F_LAG) & (first < EARLY_Z + 2 * F_LAG), to_partner, first - 2 * F_LAG)

    lane = lax.broadcasted_iota(jnp.int32, (8, LANES), 1)

    def gather(blocks, stride):
        return sum(jnp.where((lane // stride) % 4 == i, blocks[i], 0) for i in range(4))

    for group, sem in ((mates, 0), (others, 1)):
        for peer in group:
            block = derivs.at[0, 0, peer[2] // 2, pl.ds(peer[3] * 2, 2)]
            send(block, r0.at[core, z], s_r.at[sem], r_sem.at[0], peer)
    keep(derivs.at[0, 0, z // 2, pl.ds(core * 2, 2)], r0.at[core, z], r_sem.at[0])
    to_x(EARLY_Z)
    for peer in mates:
        send(energy.at[0], ez.at[z], s_e.at[0], e_sem.at[0], peer)
    keep(energy.at[0], ez.at[z], e_sem.at[0])
    pl.loop(EARLY_Z + 1, EARLY_Z + AT_ONCE)(to_x)

    with jax.named_scope("r1"):
        await_bytes(r0, r_sem.at[0])
        for peer in along_x:
            send(r0.at[:, :, 0], ra.at[y, x], s_r.at[2], r_sem.at[1], peer)
        keep(r0.at[:, :, 0], ra.at[y, x], r_sem.at[1])
        for peer in along_y:
            send(r0.at[:, :, 1], rb.at[x, y], s_r.at[3], r_sem.at[2], peer)
        keep(r0.at[:, :, 1], rb.at[x, y], r_sem.at[2])
    for k in range(EARLY_Z):
        first_z(k)
    to_y(EARLY_Z)
    pl.loop(EARLY_Z + AT_ONCE, EARLY_Z + AHEAD + 1)(to_x)
    to_y(EARLY_Z + 1)
    to_x(EARLY_Z + AHEAD + 1)
    await_bytes(ez, e_sem.at[0])
    energy[1] = gather(ez, 32)
    to_z(EARLY_Z)
    with jax.named_scope("r2"):
        await_bytes(ra.at[y], r_sem.at[1])
        await_bytes(rb.at[x], r_sem.at[2])
        for piece in range(SLAB_FIRST):
            slab_direct(piece)
    to_y(EARLY_Z + 2)
    to_x(EARLY_Z + AHEAD + 2)
    to_z(EARLY_Z + 1)
    slab_direct(SLAB_FIRST)
    for peer in along_x:
        send(energy.at[1], ex.at[x], s_e.at[1], e_sem.at[1], peer)
    keep(energy.at[1], ex.at[x], e_sem.at[1])
    middle = 6
    pl.loop(3, middle)(step)
    await_bytes(ex, e_sem.at[1])
    energy[2] = gather(ex, 8)
    step(middle)
    for peer in along_y:
        send(energy.at[2], ey.at[y], s_e.at[2], e_sem.at[2], peer)
    keep(energy.at[2], ey.at[y], e_sem.at[2])
    pl.loop(middle + 1, FIRST - 1)(step)
    with jax.named_scope("e"):
        await_bytes(ey, e_sem.at[2])
        energy[3] = gather(ey, 2)
    step(FIRST - 1)
    send(energy.at[3], energy.at[4], s_e.at[3], e_sem.at[3], partner)

    with jax.named_scope("r3"):
        await_bytes(ra.at[0], r_sem.at[3])
        await_bytes(rb.at[0], r_sem.at[4])

    @pl.loop(0, quarter)
    @jax.named_scope("prep")
    def _(c):
        for half, source in enumerate((ra, rb)):
            blocks = []
            for i in range(8):
                block = source[:, :, i // 4, i % 4, c].astype(F32)
                if half == 1:
                    block = jnp.stack([block[:, j] for j in range(4)])
                blocks.append(block.reshape(128, LANES))
            total = sum(b.reshape(16, 8, LANES).sum(axis=0) for b in blocks)
            mean = total.sum(axis=0, keepdims=True) / 1024
            rows = pl.ds(pl.multiple_of((half * quarter + c) * LANES, LANES), LANES)
            for i, block in enumerate(blocks):
                row_t[rows, i * 128 : (i + 1) * 128] = (block - mean).T.astype(BF16)

    with jax.named_scope("w"):
        await_bytes(energy.at[4], e_sem.at[3])
        every = jnp.where(lane % 2 == core, energy[3], energy[4])
        every = every - every.sum(axis=0, keepdims=True).sum(axis=1, keepdims=True) / 1024
        for i in range(128):
            at = (i // 16 % 4) * 32 + (i % 4) * 8 + (i // 4 % 4) * 2 + i // 64
            weight[i * 8 : i * 8 + 8, :] = jnp.broadcast_to(every[:, at : at + 1], (8, LANES))

    @pl.loop(FIRST, rest + LAG_Y + LAG_Z)
    def _(i):
        step(i)
        pl.loop(finished(i - 1), finished(i))(finish)

    pl.loop(finished(chunks + LAG_Y + LAG_Z - 1), early)(finish)
    pl.loop(early, chunks)(lambda k: await_bytes(tiles.at[k, 1 - core], c_sem.at[k]))

    await_bytes(zb.at[:, 0:3], s_f.at[0])
    await_bytes(fb.at[:, 0:3], s_f.at[1])
    await_bytes(fb.at[:, 0:3], s_f.at[2])
    await_bytes(xb.at[EARLY_Z:, :, 0:3], s_x)
    await_bytes(yb.at[EARLY_Z:, :, 0:3], s_y)
    await_bytes(tiles.at[EARLY_Z:, 0, 0:3], s_z)
    await_bytes(tiles.at[:, 0], s_c)
    await_bytes(r0.at[0, 0:3], s_r.at[0])
    await_bytes(r0.at[0], s_r.at[1])
    await_bytes(ra.at[0, 0:3], s_r.at[2])
    await_bytes(rb.at[0, 0:3], s_r.at[3])
    await_bytes(ra.at[0:2], s_r.at[4])
    await_bytes(rb.at[0:2], s_r.at[5])
    await_bytes(ra.at[0], s_r.at[6])
    await_bytes(rb.at[0], s_r.at[7])
    await_bytes(ez.at[0:3], s_e.at[0])
    await_bytes(ex.at[0:3], s_e.at[1])
    await_bytes(ey.at[0:3], s_e.at[2])
    await_bytes(energy.at[3], s_e.at[3])


def write(tiles, row_t, weight, done, corr, hamil, late, mixed, sem):
    chunks, early = tiles.shape[0], done.shape[0]
    outs = (corr, hamil)

    def put(source, k):
        for a, out in enumerate(outs):
            columns = pl.ds(pl.multiple_of(k * LANES, LANES), LANES)
            keep(source.at[:, a * LANES : (a + 1) * LANES], out.at[:, columns], sem.at[a])

    pl.loop(0, early)(lambda k: put(done.at[k], k))

    @pl.loop(early, chunks)
    def _(k):
        def store(rows, value):
            late[k - early, rows, :] = value

        multiply(k, tiles, row_t, weight, mixed, store)
        put(late.at[k - early], k)

    for a, out in enumerate(outs):
        await_bytes(out, sem.at[a])


def body(derivs, grads, energies):
    chunks = 2048 // WIDTH
    early = chunks - TAIL
    quarter = chunks // 4

    def view(a):
        a = a.reshape(8, 2, 4, 4, 4, quarter, WIDTH).transpose(1, 2, 3, 4, 5, 0, 6)
        return pltpu.with_memory_space_constraint(a, pltpu.HBM)

    hbm = pl.BlockSpec(memory_space=pltpu.HBM)
    vmem = pl.BlockSpec(memory_space=pltpu.VMEM)
    dma = pltpu.SemaphoreType.DMA
    tiles, row_t, weight, done = pl.pallas_call(
        exchange,
        out_shape=(
            pltpu.VMEM((chunks, 2, 4, 4, 2, 4, 8, WIDTH), BF16),
            pltpu.VMEM((1024, 1024), BF16),
            pltpu.VMEM((1024, LANES), F32),
            pltpu.VMEM((early, 1024, 2 * WIDTH), F32),
        ),
        in_specs=[hbm, hbm, vmem],
        out_specs=(vmem,) * 4,
        scratch_shapes=[
            pltpu.VMEM((5, 8, LANES), F32),
            pltpu.VMEM((EARLY_Z, 4, 4, 4, 2, 8, WIDTH), BF16),
            pltpu.VMEM((EARLY_Z, 4, 4, 2, 4, 8, WIDTH), BF16),
            pltpu.VMEM((chunks, 2, 4, 2, 4, 8, WIDTH), BF16),
            pltpu.VMEM((chunks, 2, 4, 2, 4, 8, WIDTH), BF16),
            pltpu.VMEM((2, 4, 2, quarter, 8, WIDTH), BF16),
            pltpu.VMEM((4, 4, 2, 4, quarter, 8, WIDTH), BF16),
            pltpu.VMEM((4, 4, 2, 4, quarter, 8, WIDTH), BF16),
            pltpu.VMEM((4, 8, LANES), F32),
            pltpu.VMEM((4, 8, LANES), F32),
            pltpu.VMEM((4, 8, LANES), F32),
            pltpu.VMEM((1024, 2 * WIDTH), BF16),
            dma((3,)), dma, dma, dma, dma, dma((8,)), dma((4,)), dma((EARLY_Z,)), dma((EARLY_Z,)), dma((2, 8)),
            dma((chunks,)), dma((chunks,)), dma((chunks,)), dma((chunks,)), dma((5,)), dma((4,)),
        ],
        compiler_params=pltpu.CompilerParams(
            collective_id=0, has_side_effects=True, vmem_limit_bytes=20 << 20
        ),
        name="exchange",
    )(view(derivs), view(grads), energies.reshape(1, 8))
    out = jax.ShapeDtypeStruct((1024, 2048), F32)
    return pl.pallas_call(
        write,
        out_shape=(out, out),
        in_specs=[vmem] * 4,
        out_specs=(hbm, hbm),
        scratch_shapes=[
            pltpu.VMEM((TAIL, 1024, 2 * WIDTH), F32),
            pltpu.VMEM((1024, 2 * WIDTH), BF16),
            dma((2,)),
        ],
        compiler_params=pltpu.CompilerParams(vmem_limit_bytes=8 << 20),
        name="write",
    )(tiles, row_t, weight, done)


def solution(mesh):
    placed = (P(("row", "col"), None), P(("row", "col"), None), P(("row", "col")))
    return jax.shard_map(
        body,
        mesh=mesh,
        in_specs=placed,
        out_specs=(P("row", "col"), P("row", "col")),
        check_vma=False,
    )
```
